32 devices in a mesh: space: 2 (over y), inner: 16 (over z, x, core).
Axes of the slice: x: 2, y: 2, z: 4, core: 2. Of those that a mesh axis runs over, the one named last changes fastest.
Arguments:
- hamiltonian: bfloat16 [64, 5, 128, 128], P(('space', 'inner')), as said below
- pattern: int32 [64, 5], P(('space', 'inner')), may hold values from 0 to 1, as said below
- ortho: bfloat16 [64, 2, 128, 128], P(('space', 'inner')), may hold values from -0.25 to 0.25
- lists: int32 [64, 6], P(('space', 'inner')), may hold values from -1 to 63, as said below
Outputs:
- density: float32 [64, 13, 128, 128], P(('space', 'inner'))
The draws below stay inside these ranges and needn't reach their ends.
Inputs may be any that keep to these rules, and one draw needn't show every extreme that they name: Symmetric block band: hamiltonian[j, r] is the transpose of hamiltonian[j + r - 2, 4 - r]; blocks that point outside the matrix are zero. symmetric: pattern[j, r] equals pattern[j + r - 2, 4 - r]; the middle entry is 1; entries that point outside the matrix are 0. lists[j, 0] = j; the next entries are distinct block columns within 5 of j other than j, followed only by -1; each row has 3 to 6 entries that are not -1, and some row has 6.
All inputs are finite; a program needn't handle non-finite values.
Results may differ from the reference program's by a relative error of at most 0.0055.
Values may be sent and summed in bfloat16 or wider, within the bound.
A program may use at most 64 MiB of HBM per device.

```python
import math
import jax
import jax.numpy as jnp
import numpy as np
from jax import lax

BS = 128
RH = 2
RO = 3
Q = 5
KMAX = 6
KMIN = 3
STEPS = 3
NB = 64


def draw_hamiltonian(key, part):
    band_width = 2 * RH + 1
    raw_values = jax.random.normal(key, (NB, band_width, BS, BS), jnp.float32)
    raw_values = raw_values / math.sqrt(band_width * BS)
    col_index = jnp.arange(NB)[:, None]
    band_index = jnp.arange(band_width)[None, :]
    row_index = col_index + band_index - RH
    inside = (row_index >= 0) & (row_index < NB)
    partner = raw_values[jnp.clip(row_index, 0, NB - 1), 2 * RH - band_index]
    symmetric = 0.5 * (raw_values + jnp.swapaxes(partner, -1, -2))
    return jnp.where(inside[:, :, None, None], symmetric, 0.0).astype(jnp.bfloat16)


def draw_pattern(key, part):
    band_width = 2 * RH + 1
    key = jax.random.fold_in(key, 11)
    marks = (jax.random.randint(key, (NB, band_width), 0, 10) < 7).astype(jnp.int32)
    col_index = jnp.arange(NB)[:, None]
    band_index = jnp.arange(band_width)[None, :]
    row_index = col_index + band_index - RH
    inside = (row_index >= 0) & (row_index < NB)
    partner = marks[jnp.clip(row_index, 0, NB - 1), 2 * RH - band_index]
    joined = jnp.maximum(marks, partner)
    joined = jnp.where(band_index == RH, 1, joined)
    return jnp.where(inside, joined, 0).astype(jnp.int32)


def draw_lists(key, part):
    key = jax.random.fold_in(key, 23)
    first_key, second_key = jax.random.split(key)
    candidates = jnp.concatenate([jnp.arange(-Q, 0), jnp.arange(1, Q + 1)])
    col_index = jnp.arange(NB)
    targets = col_index[:, None] + candidates[None, :]
    inside = (targets >= 0) & (targets < NB)
    scores = jax.random.randint(first_key, (NB, 2 * Q), 0, 1 << 20) * (2 * Q) + jnp.arange(2 * Q)[None, :]
    scores = scores + jnp.where(inside, 0, 1 << 26)
    ranking = jnp.argsort(scores, axis=1)
    chosen = jnp.take_along_axis(targets, ranking, 1)[:, :KMAX - 1]
    counts = jax.random.randint(second_key, (NB,), KMIN, KMAX + 1)
    counts = jnp.where(col_index == NB // 2, KMAX, counts)
    slot_index = jnp.arange(KMAX - 1)[None, :]
    others = jnp.where(slot_index < counts[:, None] - 1, chosen, -1)
    return jnp.concatenate([col_index[:, None], others], 1).astype(jnp.int32)


def steps_of(rng, dims, cuts, low, top_value):
    loudness, own = 1.0, jax.random.fold_in(rng, 6)
    for axis_at, blocks in cuts:
        draws = jnp.exp(jax.random.uniform(jax.random.fold_in(own, axis_at), (blocks,), jnp.float32, low / len(cuts), top_value / len(cuts)))
        loudness = loudness * jnp.repeat(draws, dims[axis_at] // blocks).reshape([-1 if axis == axis_at else 1 for axis in range(len(dims))])
    return loudness


def noise(key, extent, scale, bound, cuts=(), kind=jnp.bfloat16):
    entries = scale * jax.random.normal(key, extent, jnp.float32)
    if cuts:
        entries = entries * steps_of(key, extent, cuts, -0.22, 0.18)
    return jnp.clip(entries, -bound, bound).astype(kind)


def setup_inputs(seed: int = 0) -> dict:
    splits = jax.random.split(jax.random.key(seed), 5)
    hamiltonian = draw_hamiltonian(jax.random.fold_in(splits[4], 71), 0)
    pattern = draw_pattern(jax.random.fold_in(splits[4], 71), 0)
    ortho = noise(splits[2], (NB, 2, BS, BS), (4 * BS) ** -0.5, 0.25, ((0, 32),))
    lists = draw_lists(jax.random.fold_in(splits[4], 71), 0)
    return dict(hamiltonian=hamiltonian, pattern=pattern, ortho=ortho, lists=lists)


chem_level = 0.25

def orth_columns(ham_ext, ortho_ext, ham_off, ortho_off, count):
    column_range = np.arange(count)
    previous = ham_ext[ham_off + column_range - 1].astype(jnp.float32)
    current = ham_ext[ham_off + column_range].astype(jnp.float32)
    upper = ortho_ext[ortho_off + column_range, 0].astype(jnp.float32)
    diagonal = ortho_ext[ortho_off + column_range, 1].astype(jnp.float32)
    row_index = ortho_off + column_range[:, None] + np.arange(-RO, RO + 1)[None, :]
    z_rows = ortho_ext[row_index].astype(jnp.float32)
    left_padded = jnp.pad(previous, ((0, 0), (1, 2), (0, 0), (0, 0)))
    right_padded = jnp.pad(current, ((0, 0), (2, 1), (0, 0), (0, 0)))
    product = jnp.einsum('cgab,cbd->cgad', left_padded, upper, precision=lax.Precision.HIGHEST)
    product = product + jnp.einsum('cgab,cbd->cgad', right_padded, diagonal, precision=lax.Precision.HIGHEST)
    product = lax.optimization_barrier(product.astype(jnp.bfloat16)).astype(jnp.float32)
    result = jnp.einsum('cqba,cqbd->cqad', z_rows[:, :, 0], product[:, :-1], precision=lax.Precision.HIGHEST)
    result = result + jnp.einsum('cqba,cqbd->cqad', z_rows[:, :, 1], product[:, 1:], precision=lax.Precision.HIGHEST)
    return result.astype(jnp.bfloat16)

def mat_product(left, right):
    return jnp.dot(left.astype(jnp.float32), right.astype(jnp.float32), precision=lax.Precision.HIGHEST)

def solve_column(orth_ext, base, slots, column):
    slots = slots.astype(jnp.int32)
    positions = jnp.clip(slots - base, 0, orth_ext.shape[0] - 1).astype(jnp.int32)
    gathered = orth_ext[positions].astype(jnp.float32)
    first_row = 2 * RO + 1 - gathered.shape[1]
    live = slots >= 0
    both_live = live[:, None, None] & live[None, :, None]
    offsets_grid = slots[:, None] - slots[None, :] + RO
    band_rows = jnp.arange(first_row, 2 * RO + 1, dtype=jnp.int32)[None, None, :]
    lower_sel = (offsets_grid[:, :, None] == band_rows) & (offsets_grid >= RO)[:, :, None] & both_live
    upper_sel = ((2 * RO - offsets_grid)[:, :, None] == band_rows) & (offsets_grid < RO)[:, :, None] & both_live
    sub_block = jnp.einsum('str,trab->satb', lower_sel.astype(jnp.float32), gathered, precision=lax.Precision.HIGHEST)
    sub_block = sub_block + jnp.einsum('str,srba->satb', upper_sel.astype(jnp.float32), gathered, precision=lax.Precision.HIGHEST)
    slot_count = gathered.shape[0]
    block_size = gathered.shape[-1]
    order_n = slot_count * block_size
    sub_block = sub_block.reshape(order_n, order_n)
    diag_values = jnp.repeat(live.astype(jnp.float32), block_size)
    shifted = chem_level * jnp.diag(diag_values) - sub_block
    squares = jnp.sum(shifted * shifted)
    live_rows = jnp.sum(live.astype(jnp.float32)) * block_size
    scale = 2.0 * jnp.sqrt(squares / live_rows + 1e-06)
    iterate = (shifted / scale).astype(jnp.bfloat16)
    identity = jnp.eye(order_n, dtype=jnp.float32)
    for step_index in range(STEPS - 1):
        square = mat_product(iterate, iterate)
        factor = (1.5 * identity - 0.5 * square).astype(jnp.bfloat16)
        iterate = mat_product(iterate, factor).astype(jnp.bfloat16)
    columns = iterate[:, :block_size]
    unit = identity[:, :block_size]
    square_col = mat_product(iterate, columns)
    factor_col = (1.5 * unit - 0.5 * square_col).astype(jnp.bfloat16)
    result = mat_product(iterate, factor_col)
    pcol = (0.5 * (unit + result)).reshape(slot_count, block_size, block_size)
    placing = (((slots - column + Q)[:, None] == jnp.arange(2 * Q + 1, dtype=jnp.int32)[None, :]) & live[:, None]).astype(jnp.float32)
    return jnp.einsum('sr,sab->rab', placing, pcol, precision=lax.Precision.HIGHEST)

def back_transform(porth, porth_next, ortho_ext, ortho_off, count):
    column_range = np.arange(count)
    diag_own = ortho_ext[ortho_off + column_range, 1].astype(jnp.float32)
    upper_next = ortho_ext[ortho_off + column_range + 1, 0].astype(jnp.float32)
    low_band = jnp.pad(porth, ((0, 0), (0, 1), (0, 0), (0, 0)))
    high_band = jnp.pad(porth_next, ((0, 0), (1, 0), (0, 0), (0, 0)))
    right_part = jnp.einsum('crab,cdb->crad', low_band, diag_own, precision=lax.Precision.HIGHEST)
    right_part = right_part + jnp.einsum('crab,cdb->crad', high_band, upper_next, precision=lax.Precision.HIGHEST)
    row_index = ortho_off + column_range[:, None] + np.arange(-Q - 1, Q + 2)[None, :]
    diag_rows = ortho_ext[row_index, 1].astype(jnp.float32)
    upper_rows = ortho_ext[row_index + 1, 0].astype(jnp.float32)
    lower_y = jnp.pad(right_part, ((0, 0), (1, 0), (0, 0), (0, 0)))
    upper_y = jnp.pad(right_part, ((0, 0), (0, 1), (0, 0), (0, 0)))
    result = jnp.einsum('cpab,cpbd->cpad', diag_rows, lower_y, precision=lax.Precision.HIGHEST)
    return result + jnp.einsum('cpab,cpbd->cpad', upper_rows, upper_y, precision=lax.Precision.HIGHEST)

def reference(hamiltonian, pattern, ortho, lists):
    total = hamiltonian.shape[0]
    block_size = hamiltonian.shape[-1]
    masked = hamiltonian * pattern[:, :, None, None].astype(jnp.bfloat16)
    index_all = jnp.arange(total, dtype=jnp.int32)
    upper = jnp.where((index_all == 0)[:, None, None], jnp.zeros_like(ortho[:, 0]), ortho[:, 0])
    diag_z = (jnp.eye(block_size, dtype=jnp.float32) + ortho[:, 1].astype(jnp.float32)).astype(jnp.bfloat16)
    stacked = jnp.stack([upper, diag_z], 1)
    margin = Q + RO + 2
    ortho_ext = jnp.pad(stacked, ((margin, margin), (0, 0), (0, 0), (0, 0)))
    ham_ext = jnp.pad(masked, ((1, 0), (0, 0), (0, 0), (0, 0)))
    ham_orth = orth_columns(ham_ext, ortho_ext, 1, margin, total)
    orth_ext = jnp.pad(ham_orth, ((Q, Q), (0, 0), (0, 0), (0, 0)))
    bands = lax.map(lambda item: solve_column(orth_ext, -Q, item[0], item[1]), (lists, index_all))
    following = jnp.concatenate([bands[1:], jnp.zeros_like(bands[:1])], 0)
    return back_transform(bands, following, ortho_ext, margin, total)
```

```python
import functools
import math

import jax
import jax.numpy as jnp
from jax import lax
from jax.experimental import pallas as pl
from jax.experimental.pallas import tpu as pltpu
from jax.sharding import PartitionSpec as P

RO = 3
Q = 5
STEPS = 3
CHEM = 0.25
AXES = ("space", "inner")
MESH = pl.DeviceIdType.MESH
BF = jnp.bfloat16
F32 = jnp.float32
PER = 5
REACH = 3
HALF = 5
VMEM_LIMIT = 60 * 1024 * 1024


def gather_kernel(total, inner, pay_ref, out_ref, own_sem, send_sem, recv_sem):
    me = lax.axis_index("space") * inner + lax.axis_index("inner")
    core = lax.rem(me, 2)
    partner = me + 1 - 2 * core
    far = jnp.where(core == 1, me + 3, me - 3)
    has_low = me >= 2
    has_high = me + 2 < total
    has_far = (far >= 0) & (far < total)

    def place(device):
        return (device // inner, lax.rem(device, inner))

    barrier = pltpu.get_barrier_semaphore()

    def greet(device):
        pl.semaphore_signal(barrier, inc=1, device_id=place(device), device_id_type=MESH)

    greet(partner)
    pl.when(has_low)(lambda: greet(me - 2))
    pl.when(has_high)(lambda: greet(me + 2))
    pl.when(has_far)(lambda: greet(far))

    own = pltpu.make_async_copy(pay_ref, out_ref.at[REACH], own_sem)
    own.start()
    for slot in range(2 * REACH + 1):
        if slot != REACH:
            source = me + slot - REACH

            @pl.when((source < 0) | (source >= total))
            def _():
                out_ref[slot] = jnp.zeros(out_ref.shape[1:], out_ref.dtype)

    peers = 1 + has_low.astype(jnp.int32) + has_high.astype(jnp.int32) + has_far.astype(jnp.int32)
    pl.semaphore_wait(barrier, peers)

    def copy(src, dst_slot, lo, hi, number, part, device):
        return pltpu.make_async_remote_copy(
            src_ref=src.at[pl.ds(lo, hi - lo)],
            dst_ref=out_ref.at[dst_slot, pl.ds(lo, hi - lo)],
            send_sem=send_sem.at[number, part],
            recv_sem=recv_sem.at[dst_slot, part],
            device_id=place(device),
            device_id_type=MESH,
        )

    halves = ((0, 0, HALF), (1, HALF, 2 * HALF))

    up = [copy(pay_ref, 1, lo, hi, 0, part, me + 2) for part, lo, hi in halves]
    down = [copy(pay_ref, 5, lo, hi, 1, part, me - 2) for part, lo, hi in halves]
    far_up = [copy(pay_ref, 0, lo, hi, 2, part, far) for part, lo, hi in ((0, 2, HALF), (1, HALF, 10))]
    far_down = [copy(pay_ref, 6, lo, hi, 2, part, far) for part, lo, hi in ((0, 0, HALF), (1, HALF, 7))]
    side_up = [copy(pay_ref, 2, lo, hi, 3, part, partner) for part, lo, hi in halves]
    side_down = [copy(pay_ref, 4, lo, hi, 3, part, partner) for part, lo, hi in halves]
    low0 = [copy(out_ref.at[1], 0, lo, hi, 4, part, partner) for part, lo, hi in ((0, 2, HALF), (1, HALF, 10))]
    low1 = [copy(out_ref.at[1], 2, lo, hi, 4, part, partner) for part, lo, hi in halves]
    high0 = [copy(out_ref.at[5], 4, lo, hi, 5, part, partner) for part, lo, hi in halves]
    high1 = [copy(out_ref.at[5], 6, lo, hi, 5, part, partner) for part, lo, hi in ((0, 0, HALF), (1, HALF, 7))]

    even = core == 0
    odd = core == 1
    for part in range(2):
        pl.when(has_high)(lambda: up[part].start())
        pl.when(has_low)(lambda: down[part].start())
        pl.when(has_far & odd)(lambda: far_up[part].start())
        pl.when(has_far & even)(lambda: far_down[part].start())
        pl.when(even)(lambda: side_up[part].start())
        pl.when(odd)(lambda: side_down[part].start())

    for part in range(2):

        @pl.when(has_low)
        def _():
            up[part].wait_recv()
            pl.when(even)(lambda: low0[part].start())
            pl.when(odd)(lambda: low1[part].start())

        @pl.when(has_high)
        def _():
            down[part].wait_recv()
            pl.when(even)(lambda: high0[part].start())
            pl.when(odd)(lambda: high1[part].start())

    for part in range(2):

        @pl.when(even)
        def _():
            pl.when(has_far)(lambda: far_up[part].wait_recv())
            pl.when(has_low)(lambda: low1[part].wait_recv())
            side_down[part].wait_recv()
            pl.when(has_high)(lambda: high1[part].wait_recv())
            pl.when(has_far)(lambda: far_down[part].wait_send())
            side_up[part].wait_send()
            pl.when(has_low)(lambda: low0[part].wait_send())
            pl.when(has_high)(lambda: high0[part].wait_send())

        @pl.when(odd)
        def _():
            pl.when(has_low)(lambda: low0[part].wait_recv())
            side_up[part].wait_recv()
            pl.when(has_high)(lambda: high0[part].wait_recv())
            pl.when(has_far)(lambda: far_down[part].wait_recv())
            pl.when(has_far)(lambda: far_up[part].wait_send())
            side_down[part].wait_send()
            pl.when(has_low)(lambda: low1[part].wait_send())
            pl.when(has_high)(lambda: high1[part].wait_send())

        pl.when(has_high)(lambda: up[part].wait_send())
        pl.when(has_low)(lambda: down[part].wait_send())
    own.wait()


def gather(payload, total, inner):
    shape = (2 * REACH + 1,) + payload.shape
    return pl.pallas_call(
        functools.partial(gather_kernel, total, inner),
        out_shape=jax.ShapeDtypeStruct(shape, payload.dtype),
        in_specs=[pl.BlockSpec(memory_space=pltpu.VMEM)],
        out_specs=pl.BlockSpec(memory_space=pltpu.VMEM),
        scratch_shapes=[
            pltpu.SemaphoreType.DMA,
            pltpu.SemaphoreType.DMA((6, 2)),
            pltpu.SemaphoreType.DMA((2 * REACH + 1, 2)),
        ],
        compiler_params=pltpu.CompilerParams(collective_id=0, has_side_effects=True),
        name="gather",
    )(payload)


def block_of(g_ref, column, which):
    index = column + 2 * REACH
    return g_ref[index // 2, (index % 2) * PER + which]


def dot(left, right):
    return jnp.dot(left, right, preferred_element_type=F32)


def eye_mask(rows, columns, shift=0):
    row = lax.broadcasted_iota(jnp.int32, (rows, columns), 0) + shift
    return row == lax.broadcasted_iota(jnp.int32, (rows, columns), 1)


def fold(square):
    n = square.shape[0]
    return jnp.sum(square.reshape(n // 8, 8, square.shape[1]), axis=0)


def orth_stage(g_ref, h_ref, sq_ref, zt_ref):
    bs = g_ref.shape[-1]
    last = Q + 1
    quarter = jnp.where(eye_mask(bs, bs), CHEM, 0.0)
    for a in range(-Q, last + 1):
        zt_ref[a + Q] = jnp.concatenate(
            [block_of(g_ref, a, 0).T, block_of(g_ref, a, 1).T], axis=1
        )
    for b in range(-Q, last + 1):
        count = min(RO + 1, last - b + 1)
        z_col = jnp.concatenate([block_of(g_ref, b, 0), block_of(g_ref, b, 1)], axis=0)
        below = block_of(g_ref, b - 1, 3)
        rows = [jnp.concatenate([block_of(g_ref, b - 1, 2), below.T], axis=1)]
        rows.append(jnp.concatenate([below, block_of(g_ref, b, 2)], axis=1))
        if count >= 2:
            rows.append(jnp.concatenate([block_of(g_ref, b - 1, 4), block_of(g_ref, b, 3)], axis=1))
        product = dot(jnp.concatenate(rows, axis=0), z_col).astype(BF)
        if count >= 3:
            tail = dot(block_of(g_ref, b, 4), z_col[bs:]).astype(BF)
            product = jnp.concatenate([product, tail], axis=0)
        for off in range(count):
            transposed = zt_ref[b + off + Q]
            if off < RO:
                value = dot(transposed, product[off * bs : (off + 2) * bs])
            else:
                value = dot(transposed[:, :bs], product[off * bs : (off + 1) * bs])
            value = value.astype(BF)
            h_ref[b + Q, off] = value
            wide = value.astype(F32)
            if off == 0:
                wide = quarter - wide
            sq_ref[b + Q, off] = fold(wide * wide)


def solve_stage(which, lists_ref, first, h_ref, sq_ref, band_ref, x_ref, m_ref, y_ref):
    bs = h_ref.shape[-1]
    slot_count = lists_ref.shape[1]
    order = slot_count * bs
    slots = [lists_ref[which, s] for s in range(slot_count)]
    live = [slot >= 0 for slot in slots]
    place = [jnp.clip(slot - first + Q, 0, 2 * Q + 1) for slot in slots]
    total = jnp.zeros((8, bs), F32)
    live_count = jnp.int32(0)
    pick = {}
    for s in range(slot_count):
        live_count = live_count + live[s].astype(jnp.int32)
        for t in range(s + 1):
            low = jnp.minimum(place[s], place[t])
            off = jnp.maximum(place[s], place[t]) - low
            valid = live[s] & live[t] & (off <= RO)
            off = jnp.minimum(off, RO)
            pick[s, t] = (low, off, valid)
            part = jnp.where(valid, sq_ref[low, off], 0.0)
            total = total + (part if s == t else 2.0 * part)
    total = jnp.sum(jnp.sum(total, axis=1, keepdims=True), axis=0, keepdims=True)
    rows = jnp.full((1, 1), live_count * bs, jnp.int32).astype(F32)
    scale = 2.0 * jnp.sqrt(total / rows + 1e-06)
    inverse = 1.0 / scale
    eye = eye_mask(bs, bs)
    for s in range(slot_count):
        for t in range(s + 1):
            low, off, valid = pick[s, t]
            value = h_ref[low, off].astype(F32)
            if s == t:
                value = jnp.where(eye, CHEM, 0.0) - value
            else:
                value = -value
            value = jnp.where(valid, value * inverse, 0.0)
            here, there = pl.ds(s * bs, bs), pl.ds(t * bs, bs)
            if s == t:
                x_ref[here, here] = value.astype(BF)
            else:
                flipped = value.T
                straight = place[s] >= place[t]
                x_ref[here, there] = jnp.where(straight, value, flipped).astype(BF)
                x_ref[there, here] = jnp.where(straight, flipped, value).astype(BF)
    chunk = math.gcd(order, 256)
    source, target = x_ref, y_ref
    for step in range(STEPS - 1):
        for at in range(0, order, chunk):
            square = dot(source[pl.ds(at, chunk), :], source[...])
            unit = jnp.where(eye_mask(chunk, order, at), 1.5, 0.0)
            m_ref[pl.ds(at, chunk), :] = (unit - 0.5 * square).astype(BF)
        for at in range(0, order, chunk):
            target[pl.ds(at, chunk), :] = dot(source[pl.ds(at, chunk), :], m_ref[...]).astype(BF)
        source, target = target, source
    columns = source[:, :bs]
    for at in range(0, order, chunk):
        square = dot(source[pl.ds(at, chunk), :], columns)
        unit = jnp.where(eye_mask(chunk, bs, at), 1.5, 0.0)
        m_ref[pl.ds(at, chunk), :bs] = (unit - 0.5 * square).astype(BF)
    factor = m_ref[:, :bs]
    for r in range(2 * Q + 1):
        band_ref[r] = jnp.zeros((bs, bs), band_ref.dtype)
    for s in range(slot_count):
        result = dot(source[pl.ds(s * bs, bs), :], factor)
        if s == 0:
            result = result + jnp.where(eye, 1.0, 0.0)
        row = jnp.clip(slots[s] - first - which + Q, 0, 2 * Q)

        @pl.when(live[s])
        def _():
            band_ref[row] = (0.5 * result).astype(band_ref.dtype)


def first_index(inner, local_count):
    return (lax.axis_index("space") * inner + lax.axis_index("inner")) * local_count


def first_kernel(inner, lists_ref, g_ref, h_ref, sq_ref, band_ref, zt_ref, x_ref, m_ref, y_ref):
    orth_stage(g_ref, h_ref, sq_ref, zt_ref)
    first = first_index(inner, lists_ref.shape[0])
    solve_stage(0, lists_ref, first, h_ref, sq_ref, band_ref, x_ref, m_ref, y_ref)


def second_kernel(inner, lists_ref, h_ref, sq_ref, band_ref, x_ref, m_ref, y_ref):
    first = first_index(inner, lists_ref.shape[0])
    solve_stage(1, lists_ref, first, h_ref, sq_ref, band_ref, x_ref, m_ref, y_ref)


def back_kernel(g_ref, band0_ref, band1_ref, next_ref, out_ref):
    bs = g_ref.shape[-1]
    zero = jnp.zeros((bs, bs), BF)
    for column in range(2):
        mine = (band0_ref, band1_ref)[column]
        after = (band1_ref, next_ref)[column]
        right = jnp.concatenate(
            [block_of(g_ref, column, 1).T, block_of(g_ref, column + 1, 0).T], axis=0
        )
        rows = []
        for i in range(2 * Q + 2):
            here = mine[i] if i <= 2 * Q else zero
            there = after[i - 1] if i >= 1 else zero
            rows.append(jnp.concatenate([here, there], axis=1))
        y = dot(jnp.concatenate(rows, axis=0), right).astype(BF)
        for p in range(2 * Q + 3):
            a = column + p - Q - 1
            if p == 0:
                value = dot(block_of(g_ref, a + 1, 0), y[:bs])
            elif p == 2 * Q + 2:
                value = dot(block_of(g_ref, a, 1), y[(p - 1) * bs : p * bs])
            else:
                left = jnp.concatenate(
                    [block_of(g_ref, a, 1), block_of(g_ref, a + 1, 0)], axis=1
                )
                value = dot(left, y[(p - 1) * bs : (p + 1) * bs])
            out_ref[column, p] = value


def vmem():
    return pl.BlockSpec(memory_space=pltpu.VMEM)


def smem():
    return pl.BlockSpec(memory_space=pltpu.SMEM)


def local(total, inner, hamiltonian, pattern, ortho, lists):
    local_count, _, bs = hamiltonian.shape[:3]
    slot_count = lists.shape[1]
    order = slot_count * bs
    first = lax.axis_index(AXES) * local_count
    columns = first + jnp.arange(local_count, dtype=jnp.int32)
    masked = hamiltonian[:, 2:] * pattern[:, 2:, None, None].astype(BF)
    upper = jnp.where((columns == 0)[:, None, None], jnp.zeros_like(ortho[:, 0]), ortho[:, 0])
    diagonal = (jnp.eye(bs, dtype=F32) + ortho[:, 1].astype(F32)).astype(BF)
    payload = jnp.concatenate([upper[:, None], diagonal[:, None], masked], axis=1)
    payload = payload.reshape(local_count * PER, bs, bs)
    gathered = gather(payload, total, inner)

    params = pltpu.CompilerParams(vmem_limit_bytes=VMEM_LIMIT)
    band_shape = jax.ShapeDtypeStruct((2 * Q + 1, bs, bs), BF)
    work = [pltpu.VMEM((order, order), BF)] * 3
    orth_cols = 2 * Q + local_count
    flops = 2 * order**3 * 5
    cost = pl.CostEstimate(flops=flops, bytes_accessed=4 << 20, transcendentals=0)
    h, sq, band0 = pl.pallas_call(
        functools.partial(first_kernel, inner),
        out_shape=(
            jax.ShapeDtypeStruct((orth_cols, RO + 1, bs, bs), BF),
            jax.ShapeDtypeStruct((orth_cols, RO + 1, 8, bs), F32),
            band_shape,
        ),
        in_specs=[smem(), vmem()],
        out_specs=(vmem(), vmem(), vmem()),
        scratch_shapes=[pltpu.VMEM((orth_cols, bs, 2 * bs), BF)] + work,
        compiler_params=params,
        cost_estimate=cost,
        name="first",
    )(lists, gathered)
    devices = total
    pairs = [(i, i - 1) for i in range(1, devices)]
    following = lax.ppermute(band0, AXES, pairs)
    band1 = pl.pallas_call(
        functools.partial(second_kernel, inner),
        out_shape=band_shape,
        in_specs=[smem(), vmem(), vmem()],
        out_specs=vmem(),
        scratch_shapes=work,
        compiler_params=params,
        cost_estimate=cost,
        name="second",
    )(lists, h, sq)
    return pl.pallas_call(
        back_kernel,
        out_shape=jax.ShapeDtypeStruct((local_count, 2 * Q + 3, bs, bs), F32),
        in_specs=[vmem()] * 4,
        out_specs=vmem(),
        compiler_params=params,
        name="back",
    )(gathered, band0, band1, following)


def solution(mesh):
    in_specs = (
        P(AXES, None, None, None),
        P(AXES, None),
        P(AXES, None, None, None),
        P(AXES, None),
    )
    inner = mesh.shape["inner"]
    total = mesh.shape["space"] * inner
    return jax.shard_map(
        functools.partial(local, total, inner),
        mesh=mesh,
        in_specs=in_specs,
        out_specs=P(AXES, None, None, None),
        check_vma=False,
    )
```

```python
import functools
import math

import jax
import jax.numpy as jnp
from jax import lax
from jax.experimental import pallas as pl
from jax.experimental.pallas import tpu as pltpu
from jax.sharding import PartitionSpec as P

RO = 3
Q = 5
STEPS = 3
CHEM = 0.25
AXES = ("space", "inner")
MESH = pl.DeviceIdType.MESH
BF = jnp.bfloat16
F32 = jnp.float32
PER = 5
REACH = 3
HALF = 5
VMEM_LIMIT = 60 * 1024 * 1024


def exchange_parts(total, inner, g_ref, pay_ref, next_ref, band_ref, send_sem, recv_sem, band_sem):
    me = lax.axis_index("space") * inner + lax.axis_index("inner")
    core = lax.rem(me, 2)
    even = core == 0
    odd = core == 1
    chip_odd = lax.rem(me // 2, 2) == 1
    chip_even = lax.rem(me // 2, 2) == 0
    partner = me + 1 - 2 * core
    across = jnp.where(chip_odd, me - 2, me + 2)
    far = jnp.where(odd, me + 3, me - 3)
    side = jnp.where(odd, me + 1, me - 1)
    has_low = me >= 4
    has_high = me + 4 < total
    has_far = (far >= 0) & (far < total)
    has_side = (side >= 0) & (side < total)

    def place(device):
        return (device // inner, lax.rem(device, inner))

    def greet():
        barrier = pltpu.get_barrier_semaphore()

        def one(device):
            pl.semaphore_signal(barrier, inc=1, device_id=place(device), device_id_type=MESH)

        one(partner)
        one(across)
        pl.when(has_low)(lambda: one(me - 4))
        pl.when(has_high)(lambda: one(me + 4))
        pl.when(has_far)(lambda: one(far))
        pl.when(has_side)(lambda: one(side))

    def meet():
        peers = jnp.int32(2)
        for has in (has_low, has_high, has_far, has_side):
            peers = peers + has.astype(jnp.int32)
        pl.semaphore_wait(pltpu.get_barrier_semaphore(), peers)

    def clear():
        for slot in range(2 * REACH + 1):
            if slot != REACH:
                source = me + slot - REACH

                @pl.when((source < 0) | (source >= total))
                def _():
                    g_ref[slot] = jnp.zeros(g_ref.shape[1:], g_ref.dtype)

        @pl.when(me == total - 1)
        def _():
            next_ref[...] = jnp.zeros(next_ref.shape, next_ref.dtype)

    def copy(src, dst_slot, lo, hi, number, part, device):
        return pltpu.make_async_remote_copy(
            src_ref=src.at[pl.ds(lo, hi - lo)],
            dst_ref=g_ref.at[dst_slot, pl.ds(lo, hi - lo)],
            send_sem=send_sem.at[number, part],
            recv_sem=recv_sem.at[dst_slot, part],
            device_id=place(device),
            device_id_type=MESH,
        )

    whole = ((0, 0, HALF), (1, HALF, 2 * HALF))
    tail = ((0, 2, HALF), (1, HALF, 2 * HALF))
    head = ((0, 0, HALF), (1, HALF, HALF + 2))

    def copies(src, slot, number, device, pieces):
        return [copy(src, slot, lo, hi, number, part, device) for part, lo, hi in pieces]

    up = copies(pay_ref, 1, 0, across, whole)
    down = copies(pay_ref, 5, 0, across, whole)
    far_up = copies(pay_ref, 0, 1, far, tail)
    far_down = copies(pay_ref, 6, 1, far, head)
    side_up = copies(pay_ref, 2, 2, partner, whole)
    side_down = copies(pay_ref, 4, 2, partner, whole)
    relay_up = copies(g_ref.at[5], 1, 3, me + 4, whole)
    relay_down = copies(g_ref.at[1], 5, 3, me - 4, whole)
    low0 = copies(g_ref.at[1], 0, 4, partner, tail)
    low1 = copies(g_ref.at[1], 2, 4, partner, whole)
    high0 = copies(g_ref.at[5], 4, 5, partner, whole)
    high1 = copies(g_ref.at[5], 6, 5, partner, head)
    got_low = chip_odd | has_low
    got_high = chip_even | has_high

    def send():
        for part in range(2):
            pl.when(has_far & odd)(lambda: far_up[part].start())
            pl.when(has_far & even)(lambda: far_down[part].start())
            pl.when(chip_even)(lambda: up[part].start())
            pl.when(chip_odd)(lambda: down[part].start())
            pl.when(even)(lambda: side_up[part].start())
            pl.when(odd)(lambda: side_down[part].start())

    def pass_low(part):
        up[part].wait_recv()
        pl.when(chip_odd & has_low)(lambda: relay_down[part].start())
        pl.when(even)(lambda: low0[part].start())
        pl.when(odd)(lambda: low1[part].start())

    def pass_high(part):
        down[part].wait_recv()
        pl.when(chip_even & has_high)(lambda: relay_up[part].start())
        pl.when(even)(lambda: high0[part].start())
        pl.when(odd)(lambda: high1[part].start())

    def forward():
        for part in range(2):
            pl.when(chip_odd)(lambda: pass_low(part))
            pl.when(chip_even)(lambda: pass_high(part))
        for part in range(2):
            pl.when(chip_even & has_low)(lambda: pass_low(part))
            pl.when(chip_odd & has_high)(lambda: pass_high(part))

    def receive():
        for part in range(2):

            @pl.when(even)
            def _():
                pl.when(has_far)(lambda: far_up[part].wait_recv())
                pl.when(got_low)(lambda: low1[part].wait_recv())
                side_down[part].wait_recv()
                pl.when(got_high)(lambda: high1[part].wait_recv())

            @pl.when(odd)
            def _():
                pl.when(got_low)(lambda: low0[part].wait_recv())
                side_up[part].wait_recv()
                pl.when(got_high)(lambda: high0[part].wait_recv())
                pl.when(has_far)(lambda: far_down[part].wait_recv())

    def drain():
        for part in range(2):

            @pl.when(even)
            def _():
                pl.when(has_far)(lambda: far_down[part].wait_send())
                side_up[part].wait_send()
                pl.when(got_low)(lambda: low0[part].wait_send())
                pl.when(got_high)(lambda: high0[part].wait_send())

            @pl.when(odd)
            def _():
                pl.when(has_far)(lambda: far_up[part].wait_send())
                side_down[part].wait_send()
                pl.when(got_low)(lambda: low1[part].wait_send())
                pl.when(got_high)(lambda: high1[part].wait_send())

            pl.when(chip_even)(lambda: up[part].wait_send())
            pl.when(chip_odd)(lambda: down[part].wait_send())
            pl.when(chip_even & has_high)(lambda: relay_up[part].wait_send())
            pl.when(chip_odd & has_low)(lambda: relay_down[part].wait_send())

    band_copy = pltpu.make_async_remote_copy(
        src_ref=band_ref,
        dst_ref=next_ref,
        send_sem=band_sem.at[0],
        recv_sem=band_sem.at[1],
        device_id=place(me - 1),
        device_id_type=MESH,
    )

    def band_send():
        pl.when(me >= 1)(lambda: band_copy.start())

    def band_wait():
        pl.when(me < total - 1)(lambda: band_copy.wait_recv())
        pl.when(me >= 1)(lambda: band_copy.wait_send())

    return me, greet, meet, clear, send, forward, receive, drain, band_send, band_wait


def prepare(first, pattern_ref, ham_ref, ortho_ref, pay_ref, g_ref):
    bs = ham_ref.shape[-1]
    eye = jnp.where(eye_mask(bs, bs), 1.0, 0.0)
    for c in range(ham_ref.shape[0]):
        blocks = [
            jnp.where(first + c == 0, 0.0, ortho_ref[c, 0].astype(F32)),
            ortho_ref[c, 1].astype(F32) + eye,
        ]
        for r in range(3):
            keep = pattern_ref[c, r + 2].astype(F32)
            blocks.append(ham_ref[c, r + 2].astype(F32) * keep)
        for which, block in enumerate(blocks):
            block = block.astype(BF)
            pay_ref[c * PER + which] = block
            g_ref[REACH, c * PER + which] = block


def main_kernel(
    total,
    inner,
    lists_ref,
    pattern_ref,
    ham_ref,
    ortho_ref,
    g_ref,
    band0_ref,
    band1_ref,
    next_ref,
    pay_ref,
    h_ref,
    sq_ref,
    zt_ref,
    x_ref,
    m_ref,
    y_ref,
    pc_ref,
    send_sem,
    recv_sem,
    band_sem,
):
    me, greet, meet, clear, send, forward, receive, drain, band_send, band_wait = exchange_parts(
        total, inner, g_ref, pay_ref, next_ref, band0_ref, send_sem, recv_sem, band_sem
    )
    first = me * lists_ref.shape[0]
    greet()
    prepare(first, pattern_ref, ham_ref, ortho_ref, pay_ref, g_ref)
    clear()
    meet()
    send()
    forward()
    receive()
    orth_stage(g_ref, h_ref, sq_ref, zt_ref)
    work = (x_ref, m_ref, y_ref, pc_ref)
    assemble(0, lists_ref, first, h_ref, sq_ref, x_ref)
    iterate(0, lists_ref, first, band0_ref, *work)
    assemble(1, lists_ref, first, h_ref, sq_ref, x_ref)
    band_send()
    iterate(1, lists_ref, first, band1_ref, *work)
    drain()
    band_wait()


def block_of(g_ref, column, which):
    index = column + 2 * REACH
    return g_ref[index // 2, (index % 2) * PER + which]


def dot(left, right):
    return jnp.dot(left, right, preferred_element_type=F32)


def eye_mask(rows, columns, shift=0):
    row = lax.broadcasted_iota(jnp.int32, (rows, columns), 0) + shift
    return row == lax.broadcasted_iota(jnp.int32, (rows, columns), 1)


def fold(square):
    n = square.shape[0]
    return jnp.sum(square.reshape(n // 8, 8, square.shape[1]), axis=0)


def orth_stage(g_ref, h_ref, sq_ref, zt_ref):
    bs = g_ref.shape[-1]
    last = Q + 1
    quarter = jnp.where(eye_mask(bs, bs), CHEM, 0.0)
    for a in range(-Q, last + 1):
        zt_ref[a + Q] = jnp.concatenate(
            [block_of(g_ref, a, 0).T, block_of(g_ref, a, 1).T], axis=1
        )
    for b in range(-Q, last + 1):
        count = min(RO + 1, last - b + 1)
        z_col = jnp.concatenate([block_of(g_ref, b, 0), block_of(g_ref, b, 1)], axis=0)
        below = block_of(g_ref, b - 1, 3)
        rows = [jnp.concatenate([block_of(g_ref, b - 1, 2), below.T], axis=1)]
        rows.append(jnp.concatenate([below, block_of(g_ref, b, 2)], axis=1))
        if count >= 2:
            rows.append(jnp.concatenate([block_of(g_ref, b - 1, 4), block_of(g_ref, b, 3)], axis=1))
        product = dot(jnp.concatenate(rows, axis=0), z_col).astype(BF)
        if count >= 3:
            tail = dot(block_of(g_ref, b, 4), z_col[bs:]).astype(BF)
            product = jnp.concatenate([product, tail], axis=0)
        for off in range(count):
            transposed = zt_ref[b + off + Q]
            if off < RO:
                value = dot(transposed, product[off * bs : (off + 2) * bs])
            else:
                value = dot(transposed[:, :bs], product[off * bs : (off + 1) * bs])
            value = value.astype(BF)
            h_ref[b + Q, off] = value
            wide = value.astype(F32)
            if off == 0:
                wide = quarter - wide
            sq_ref[b + Q, off] = fold(wide * wide)


def assemble(which, lists_ref, first, h_ref, sq_ref, x_ref):
    bs = h_ref.shape[-1]
    slot_count = lists_ref.shape[1]
    slots = [lists_ref[which, s] for s in range(slot_count)]
    live = [slot >= 0 for slot in slots]
    place = [jnp.clip(slot - first + Q, 0, 2 * Q + 1) for slot in slots]
    total = jnp.zeros((8, bs), F32)
    live_count = jnp.int32(0)
    pick = {}
    for s in range(slot_count):
        live_count = live_count + live[s].astype(jnp.int32)
        for t in range(s + 1):
            low = jnp.minimum(place[s], place[t])
            off = jnp.maximum(place[s], place[t]) - low
            valid = live[s] & live[t] & (off <= RO)
            off = jnp.minimum(off, RO)
            pick[s, t] = (low, off, valid)
            part = jnp.where(valid, sq_ref[low, off], 0.0)
            total = total + (part if s == t else 2.0 * part)
    total = jnp.sum(jnp.sum(total, axis=1, keepdims=True), axis=0, keepdims=True)
    rows = jnp.full((1, 1), live_count * bs, jnp.int32).astype(F32)
    scale = 2.0 * jnp.sqrt(total / rows + 1e-06)
    inverse = 1.0 / scale
    eye = eye_mask(bs, bs)
    for s in range(slot_count):
        for t in range(s + 1):
            low, off, valid = pick[s, t]
            value = h_ref[low, off].astype(F32)
            if s == t:
                value = jnp.where(eye, CHEM, 0.0) - value
            else:
                value = -value
            value = jnp.where(valid, value * inverse, 0.0)
            here, there = pl.ds(s * bs, bs), pl.ds(t * bs, bs)
            if s == t:
                x_ref[here, here] = value.astype(BF)
            else:
                flipped = value.T
                straight = place[s] >= place[t]
                x_ref[here, there] = jnp.where(straight, value, flipped).astype(BF)
                x_ref[there, here] = jnp.where(straight, flipped, value).astype(BF)


def iterate(which, lists_ref, first, band_ref, x_ref, m_ref, y_ref, pc_ref):
    bs = pc_ref.shape[-1]
    slot_count = lists_ref.shape[1]
    order = slot_count * bs
    chunk = math.gcd(order, 256)
    source, target = x_ref, y_ref
    for step in range(STEPS - 1):
        for at in range(0, order, chunk):
            square = dot(source[pl.ds(at, chunk), :], source[...])
            unit = jnp.where(eye_mask(chunk, order, at), 1.5, 0.0)
            m_ref[pl.ds(at, chunk), :] = (unit - 0.5 * square).astype(BF)
        for at in range(0, order, chunk):
            target[pl.ds(at, chunk), :] = dot(source[pl.ds(at, chunk), :], m_ref[...]).astype(BF)
        source, target = target, source
    columns = source[:, :bs]
    for at in range(0, order, chunk):
        square = dot(source[pl.ds(at, chunk), :], columns)
        unit = jnp.where(eye_mask(chunk, bs, at), 1.5, 0.0)
        m_ref[pl.ds(at, chunk), :bs] = (unit - 0.5 * square).astype(BF)
    factor = m_ref[:, :bs]
    for s in range(slot_count):
        result = dot(source[pl.ds(s * bs, bs), :], factor)
        if s == 0:
            result = result + jnp.where(eye_mask(bs, bs), 1.0, 0.0)
        pc_ref[s] = (0.5 * result).astype(BF)
    for r in range(2 * Q + 1):
        at = jnp.int32(0)
        found = jnp.bool_(False)
        for s in range(slot_count):
            slot = lists_ref[which, s]
            hit = (slot >= 0) & (slot == first + which + r - Q)
            at = jnp.where(hit, s, at)
            found = found | hit
        band_ref[r] = jnp.where(found, pc_ref[at], jnp.zeros((bs, bs), BF))


def back_kernel(g_ref, band0_ref, band1_ref, next_ref, out_ref):
    bs = g_ref.shape[-1]
    zero = jnp.zeros((bs, bs), BF)
    for column in range(2):
        mine = (band0_ref, band1_ref)[column]
        after = (band1_ref, next_ref)[column]
        right = jnp.concatenate(
            [block_of(g_ref, column, 1).T, block_of(g_ref, column + 1, 0).T], axis=0
        )
        rows = []
        for i in range(2 * Q + 2):
            here = mine[i] if i <= 2 * Q else zero
            there = after[i - 1] if i >= 1 else zero
            rows.append(jnp.concatenate([here, there], axis=1))
        y = dot(jnp.concatenate(rows, axis=0), right).astype(BF)
        for p in range(2 * Q + 3):
            a = column + p - Q - 1
            if p == 0:
                value = dot(block_of(g_ref, a + 1, 0), y[:bs])
            elif p == 2 * Q + 2:
                value = dot(block_of(g_ref, a, 1), y[(p - 1) * bs : p * bs])
            else:
                left = jnp.concatenate(
                    [block_of(g_ref, a, 1), block_of(g_ref, a + 1, 0)], axis=1
                )
                value = dot(left, y[(p - 1) * bs : (p + 1) * bs])
            out_ref[column, p] = value


def vmem():
    return pl.BlockSpec(memory_space=pltpu.VMEM)


def smem():
    return pl.BlockSpec(memory_space=pltpu.SMEM)


def local(total, inner, hamiltonian, pattern, ortho, lists):
    local_count, _, bs = hamiltonian.shape[:3]
    slot_count = lists.shape[1]
    order = slot_count * bs
    params = pltpu.CompilerParams(vmem_limit_bytes=VMEM_LIMIT)
    band_shape = jax.ShapeDtypeStruct((2 * Q + 1, bs, bs), BF)
    orth_cols = 2 * Q + local_count
    payload = (local_count * PER, bs, bs)
    gathered, band0, band1, following = pl.pallas_call(
        functools.partial(main_kernel, total, inner),
        out_shape=(
            jax.ShapeDtypeStruct((2 * REACH + 1,) + payload, BF),
            band_shape,
            band_shape,
            band_shape,
        ),
        in_specs=[smem(), smem(), vmem(), vmem()],
        out_specs=(vmem(),) * 4,
        scratch_shapes=[
            pltpu.VMEM(payload, BF),
            pltpu.VMEM((orth_cols, RO + 1, bs, bs), BF),
            pltpu.VMEM((orth_cols, RO + 1, 8, bs), F32),
            pltpu.VMEM((orth_cols, bs, 2 * bs), BF),
            pltpu.VMEM((order, order), BF),
            pltpu.VMEM((order, order), BF),
            pltpu.VMEM((order, order), BF),
            pltpu.VMEM((slot_count, bs, bs), BF),
            pltpu.SemaphoreType.DMA((6, 2)),
            pltpu.SemaphoreType.DMA((2 * REACH + 1, 2)),
            pltpu.SemaphoreType.DMA((2,)),
        ],
        compiler_params=pltpu.CompilerParams(
            collective_id=0, has_side_effects=True, vmem_limit_bytes=VMEM_LIMIT
        ),
        name="main",
    )(lists, pattern, hamiltonian, ortho)
    return pl.pallas_call(
        back_kernel,
        out_shape=jax.ShapeDtypeStruct((local_count, 2 * Q + 3, bs, bs), F32),
        in_specs=[vmem()] * 4,
        out_specs=vmem(),
        compiler_params=params,
        name="back",
    )(gathered, band0, band1, following)


def solution(mesh):
    in_specs = (
        P(AXES, None, None, None),
        P(AXES, None),
        P(AXES, None, None, None),
        P(AXES, None),
    )
    inner = mesh.shape["inner"]
    total = mesh.shape["space"] * inner
    return jax.shard_map(
        functools.partial(local, total, inner),
        mesh=mesh,
        in_specs=in_specs,
        out_specs=P(AXES, None, None, None),
        check_vma=False,
    )
```

```python
import functools
import math

import jax
import jax.numpy as jnp
from jax import lax
from jax.experimental import pallas as pl
from jax.experimental.pallas import tpu as pltpu
from jax.sharding import PartitionSpec as P

RO = 3
Q = 5
STEPS = 3
CHEM = 0.25
AXES = ("space", "inner")
MESH = pl.DeviceIdType.MESH
BF = jnp.bfloat16
F32 = jnp.float32
PER = 5
REACH = 3
HALF = 5
VMEM_LIMIT = 60 * 1024 * 1024


def exchange_parts(total, inner, g_ref, pay_ref, next_ref, band_ref, send_sem, recv_sem, band_sem):
    me = lax.axis_index("space") * inner + lax.axis_index("inner")
    core = lax.rem(me, 2)
    even = core == 0
    odd = core == 1
    chip_odd = lax.rem(me // 2, 2) == 1
    chip_even = lax.rem(me // 2, 2) == 0
    partner = me + 1 - 2 * core
    across = jnp.where(chip_odd, me - 2, me + 2)
    far = jnp.where(odd, me + 3, me - 3)
    side = jnp.where(odd, me + 1, me - 1)
    has_low = me >= 4
    has_high = me + 4 < total
    has_far = (far >= 0) & (far < total)
    has_side = (side >= 0) & (side < total)

    def place(device):
        return (device // inner, lax.rem(device, inner))

    def greet():
        barrier = pltpu.get_barrier_semaphore()

        def one(device):
            pl.semaphore_signal(barrier, inc=1, device_id=place(device), device_id_type=MESH)

        one(partner)
        one(across)
        pl.when(has_low)(lambda: one(me - 4))
        pl.when(has_high)(lambda: one(me + 4))
        pl.when(has_far)(lambda: one(far))
        pl.when(has_side)(lambda: one(side))

    def meet():
        peers = jnp.int32(2)
        for has in (has_low, has_high, has_far, has_side):
            peers = peers + has.astype(jnp.int32)
        pl.semaphore_wait(pltpu.get_barrier_semaphore(), peers)

    def clear():
        for slot in range(2 * REACH + 1):
            if slot != REACH:
                source = me + slot - REACH

                @pl.when((source < 0) | (source >= total))
                def _():
                    g_ref[slot] = jnp.zeros(g_ref.shape[1:], g_ref.dtype)

        @pl.when(me == total - 1)
        def _():
            next_ref[...] = jnp.zeros(next_ref.shape, next_ref.dtype)

    def copy(src, dst_slot, lo, hi, number, part, device):
        return pltpu.make_async_remote_copy(
            src_ref=src.at[pl.ds(lo, hi - lo)],
            dst_ref=g_ref.at[dst_slot, pl.ds(lo, hi - lo)],
            send_sem=send_sem.at[number, part],
            recv_sem=recv_sem.at[dst_slot, part],
            device_id=place(device),
            device_id_type=MESH,
        )

    whole = ((0, 0, HALF), (1, HALF, 2 * HALF))
    tail = ((0, 2, HALF), (1, HALF, 2 * HALF))
    head = ((0, 0, HALF), (1, HALF, HALF + 2))

    def copies(src, slot, number, device, pieces):
        return [copy(src, slot, lo, hi, number, part, device) for part, lo, hi in pieces]

    up = copies(pay_ref, 1, 0, across, whole)
    down = copies(pay_ref, 5, 0, across, whole)
    far_up = copies(pay_ref, 0, 1, far, tail)
    far_down = copies(pay_ref, 6, 1, far, head)
    side_up = copies(pay_ref, 2, 2, partner, whole)
    side_down = copies(pay_ref, 4, 2, partner, whole)
    relay_up = copies(g_ref.at[5], 1, 3, me + 4, whole)
    relay_down = copies(g_ref.at[1], 5, 3, me - 4, whole)
    low0 = copies(g_ref.at[1], 0, 4, partner, tail)
    low1 = copies(g_ref.at[1], 2, 4, partner, whole)
    high0 = copies(g_ref.at[5], 4, 5, partner, whole)
    high1 = copies(g_ref.at[5], 6, 5, partner, head)
    got_low = chip_odd | has_low
    got_high = chip_even | has_high

    def send():
        for part in range(2):
            pl.when(has_far & odd)(lambda: far_up[part].start())
            pl.when(has_far & even)(lambda: far_down[part].start())
            pl.when(chip_even)(lambda: up[part].start())
            pl.when(chip_odd)(lambda: down[part].start())
            pl.when(even)(lambda: side_up[part].start())
            pl.when(odd)(lambda: side_down[part].start())

    def pass_low(part):
        up[part].wait_recv()
        pl.when(chip_odd & has_low)(lambda: relay_down[part].start())
        pl.when(even)(lambda: low0[part].start())
        pl.when(odd)(lambda: low1[part].start())

    def pass_high(part):
        down[part].wait_recv()
        pl.when(chip_even & has_high)(lambda: relay_up[part].start())
        pl.when(even)(lambda: high0[part].start())
        pl.when(odd)(lambda: high1[part].start())

    def forward():
        for part in range(2):
            pl.when(chip_odd)(lambda: pass_low(part))
            pl.when(chip_even)(lambda: pass_high(part))
        for part in range(2):
            pl.when(chip_even & has_low)(lambda: pass_low(part))
            pl.when(chip_odd & has_high)(lambda: pass_high(part))

    def receive():
        for part in range(2):

            @pl.when(even)
            def _():
                pl.when(has_far)(lambda: far_up[part].wait_recv())
                pl.when(got_low)(lambda: low1[part].wait_recv())
                side_down[part].wait_recv()
                pl.when(got_high)(lambda: high1[part].wait_recv())

            @pl.when(odd)
            def _():
                pl.when(got_low)(lambda: low0[part].wait_recv())
                side_up[part].wait_recv()
                pl.when(got_high)(lambda: high0[part].wait_recv())
                pl.when(has_far)(lambda: far_down[part].wait_recv())

    def drain():
        for part in range(2):

            @pl.when(even)
            def _():
                pl.when(has_far)(lambda: far_down[part].wait_send())
                side_up[part].wait_send()
                pl.when(got_low)(lambda: low0[part].wait_send())
                pl.when(got_high)(lambda: high0[part].wait_send())

            @pl.when(odd)
            def _():
                pl.when(has_far)(lambda: far_up[part].wait_send())
                side_down[part].wait_send()
                pl.when(got_low)(lambda: low1[part].wait_send())
                pl.when(got_high)(lambda: high1[part].wait_send())

            pl.when(chip_even)(lambda: up[part].wait_send())
            pl.when(chip_odd)(lambda: down[part].wait_send())
            pl.when(chip_even & has_high)(lambda: relay_up[part].wait_send())
            pl.when(chip_odd & has_low)(lambda: relay_down[part].wait_send())

    band_copy = pltpu.make_async_remote_copy(
        src_ref=band_ref,
        dst_ref=next_ref,
        send_sem=band_sem.at[0],
        recv_sem=band_sem.at[1],
        device_id=place(me - 1),
        device_id_type=MESH,
    )

    def band_send():
        pl.when(me >= 1)(lambda: band_copy.start())

    def band_wait():
        pl.when(me < total - 1)(lambda: band_copy.wait_recv())
        pl.when(me >= 1)(lambda: band_copy.wait_send())

    return me, greet, meet, clear, send, forward, receive, drain, band_send, band_wait


def prepare(first, pattern_ref, ham_ref, ortho_ref, pay_ref, g_ref):
    bs = ham_ref.shape[-1]
    eye = jnp.where(eye_mask(bs, bs), 1.0, 0.0)
    for c in range(ham_ref.shape[0]):
        blocks = [
            jnp.where(first + c == 0, 0.0, ortho_ref[c, 0].astype(F32)),
            ortho_ref[c, 1].astype(F32) + eye,
        ]
        for r in range(3):
            keep = pattern_ref[c, r + 2].astype(F32)
            blocks.append(ham_ref[c, r + 2].astype(F32) * keep)
        for which, block in enumerate(blocks):
            block = block.astype(BF)
            pay_ref[c * PER + which] = block
            g_ref[REACH, c * PER + which] = block


def main_kernel(
    total,
    inner,
    lists_ref,
    pattern_ref,
    ham_ref,
    ortho_ref,
    z_ref,
    band0_ref,
    band1_ref,
    next_ref,
    g_ref,
    pay_ref,
    h_ref,
    sq_ref,
    zt_ref,
    x_ref,
    m_ref,
    y_ref,
    pc_ref,
    send_sem,
    recv_sem,
    band_sem,
    z_sem,
):
    me, greet, meet, clear, send, forward, receive, drain, band_send, band_wait = exchange_parts(
        total, inner, g_ref, pay_ref, next_ref, band0_ref, send_sem, recv_sem, band_sem
    )
    first = me * lists_ref.shape[0]
    greet()
    prepare(first, pattern_ref, ham_ref, ortho_ref, pay_ref, g_ref)
    clear()
    meet()
    send()
    forward()
    receive()
    z_copies = []
    for column in range(1, z_ref.shape[0]):
        block = g_ref.at[column // 2, pl.ds((column % 2) * PER, 2)]
        z_copies.append(pltpu.make_async_copy(block, z_ref.at[column], z_sem.at[column]))
        z_copies[-1].start()
    orth_stage(g_ref, h_ref, sq_ref, zt_ref)
    work = (x_ref, m_ref, y_ref, pc_ref)
    assemble(0, lists_ref, first, h_ref, sq_ref, x_ref)
    iterate(0, lists_ref, first, band0_ref, *work)
    assemble(1, lists_ref, first, h_ref, sq_ref, x_ref)
    band_send()
    iterate(1, lists_ref, first, band1_ref, *work)
    drain()
    for z_copy in z_copies:
        z_copy.wait()
    band_wait()


def block_of(g_ref, column, which):
    index = column + 2 * REACH
    return g_ref[index // 2, (index % 2) * PER + which]


def dot(left, right):
    return jnp.dot(left, right, preferred_element_type=F32)


def eye_mask(rows, columns, shift=0):
    row = lax.broadcasted_iota(jnp.int32, (rows, columns), 0) + shift
    return row == lax.broadcasted_iota(jnp.int32, (rows, columns), 1)


def fold(square):
    n = square.shape[0]
    return jnp.sum(square.reshape(n // 8, 8, square.shape[1]), axis=0)


def orth_stage(g_ref, h_ref, sq_ref, zt_ref):
    bs = g_ref.shape[-1]
    last = Q + 1
    quarter = jnp.where(eye_mask(bs, bs), CHEM, 0.0)
    for a in range(-Q, last + 1):
        zt_ref[a + Q] = jnp.concatenate(
            [block_of(g_ref, a, 0).T, block_of(g_ref, a, 1).T], axis=1
        )
    for b in range(-Q, last + 1):
        count = min(RO + 1, last - b + 1)
        z_col = jnp.concatenate([block_of(g_ref, b, 0), block_of(g_ref, b, 1)], axis=0)
        below = block_of(g_ref, b - 1, 3)
        rows = [jnp.concatenate([block_of(g_ref, b - 1, 2), below.T], axis=1)]
        rows.append(jnp.concatenate([below, block_of(g_ref, b, 2)], axis=1))
        if count >= 2:
            rows.append(jnp.concatenate([block_of(g_ref, b - 1, 4), block_of(g_ref, b, 3)], axis=1))
        product = dot(jnp.concatenate(rows, axis=0), z_col).astype(BF)
        if count >= 3:
            tail = dot(block_of(g_ref, b, 4), z_col[bs:]).astype(BF)
            product = jnp.concatenate([product, tail], axis=0)
        for off in range(count):
            transposed = zt_ref[b + off + Q]
            if off < RO:
                value = dot(transposed, product[off * bs : (off + 2) * bs])
            else:
                value = dot(transposed[:, :bs], product[off * bs : (off + 1) * bs])
            value = value.astype(BF)
            h_ref[b + Q, off] = value
            wide = value.astype(F32)
            if off == 0:
                wide = quarter - wide
            sq_ref[b + Q, off] = fold(wide * wide)


def assemble(which, lists_ref, first, h_ref, sq_ref, x_ref):
    bs = h_ref.shape[-1]
    slot_count = lists_ref.shape[1]
    slots = [lists_ref[which, s] for s in range(slot_count)]
    live = [slot >= 0 for slot in slots]
    place = [jnp.clip(slot - first + Q, 0, 2 * Q + 1) for slot in slots]
    total = jnp.zeros((8, bs), F32)
    live_count = jnp.int32(0)
    pick = {}
    for s in range(slot_count):
        live_count = live_count + live[s].astype(jnp.int32)
        for t in range(s + 1):
            low = jnp.minimum(place[s], place[t])
            off = jnp.maximum(place[s], place[t]) - low
            valid = live[s] & live[t] & (off <= RO)
            off = jnp.minimum(off, RO)
            pick[s, t] = (low, off, valid)
            part = jnp.where(valid, sq_ref[low, off], 0.0)
            total = total + (part if s == t else 2.0 * part)
    total = jnp.sum(jnp.sum(total, axis=1, keepdims=True), axis=0, keepdims=True)
    rows = jnp.full((1, 1), live_count * bs, jnp.int32).astype(F32)
    scale = 2.0 * jnp.sqrt(total / rows + 1e-06)
    inverse = 1.0 / scale
    eye = eye_mask(bs, bs)
    for s in range(slot_count):
        for t in range(s + 1):
            low, off, valid = pick[s, t]
            value = h_ref[low, off].astype(F32)
            if s == t:
                value = jnp.where(eye, CHEM, 0.0) - value
            else:
                value = -value
            value = jnp.where(valid, value * inverse, 0.0)
            here, there = pl.ds(s * bs, bs), pl.ds(t * bs, bs)
            if s == t:
                x_ref[here, here] = value.astype(BF)
            else:
                flipped = value.T
                straight = place[s] >= place[t]
                x_ref[here, there] = jnp.where(straight, value, flipped).astype(BF)
                x_ref[there, here] = jnp.where(straight, flipped, value).astype(BF)


def iterate(which, lists_ref, first, band_ref, x_ref, m_ref, y_ref, pc_ref):
    bs = pc_ref.shape[-1]
    slot_count = lists_ref.shape[1]
    order = slot_count * bs
    chunk = math.gcd(order, 256)
    source, target = x_ref, y_ref

    def mirrored(out_ref, at, value):
        width = value.shape[1]
        out_ref[pl.ds(at, chunk), :width] = value.astype(BF)
        for left in range(0, at, chunk):
            flipped = value[:, left : left + chunk].T
            out_ref[pl.ds(left, chunk), pl.ds(at, chunk)] = flipped.astype(BF)

    for step in range(STEPS - 1):
        for at in range(0, order, chunk):
            width = at + chunk
            square = dot(source[pl.ds(at, chunk), :], source[:, :width])
            unit = jnp.where(eye_mask(chunk, width, at), 1.5, 0.0)
            mirrored(m_ref, at, unit - 0.5 * square)
        for at in range(0, order, chunk):
            mirrored(target, at, dot(source[pl.ds(at, chunk), :], m_ref[:, : at + chunk]))
        source, target = target, source
    columns = source[:, :bs]
    for at in range(0, order, chunk):
        square = dot(source[pl.ds(at, chunk), :], columns)
        unit = jnp.where(eye_mask(chunk, bs, at), 1.5, 0.0)
        m_ref[pl.ds(at, chunk), :bs] = (unit - 0.5 * square).astype(BF)
    factor = m_ref[:, :bs]
    for s in range(slot_count):
        result = dot(source[pl.ds(s * bs, bs), :], factor)
        if s == 0:
            result = result + jnp.where(eye_mask(bs, bs), 1.0, 0.0)
        pc_ref[s] = (0.5 * result).astype(BF)
    for r in range(2 * Q + 1):
        at = jnp.int32(0)
        found = jnp.bool_(False)
        for s in range(slot_count):
            slot = lists_ref[which, s]
            hit = (slot >= 0) & (slot == first + which + r - Q)
            at = jnp.where(hit, s, at)
            found = found | hit
        band_ref[r] = jnp.where(found, pc_ref[at], jnp.zeros((bs, bs), BF))


def back_kernel(z_ref, band0_ref, band1_ref, next_ref, result_ref, out_ref, out_sem):
    bs = z_ref.shape[-1]
    zero = jnp.zeros((bs, bs), BF)

    def z_of(column, which):
        return z_ref[column + 2 * REACH, which]

    sends = []
    for column in range(2):
        mine = (band0_ref, band1_ref)[column]
        after = (band1_ref, next_ref)[column]
        right = jnp.concatenate(
            [z_of(column, 1).T, z_of(column + 1, 0).T], axis=0
        )
        rows = []
        for i in range(2 * Q + 2):
            here = mine[i] if i <= 2 * Q else zero
            there = after[i - 1] if i >= 1 else zero
            rows.append(jnp.concatenate([here, there], axis=1))
        y = dot(jnp.concatenate(rows, axis=0), right).astype(BF)
        for p in range(2 * Q + 3):
            a = column + p - Q - 1
            if p == 0:
                value = dot(z_of(a + 1, 0), y[:bs])
            elif p == 2 * Q + 2:
                value = dot(z_of(a, 1), y[(p - 1) * bs : p * bs])
            else:
                left = jnp.concatenate(
                    [z_of(a, 1), z_of(a + 1, 0)], axis=1
                )
                value = dot(left, y[(p - 1) * bs : (p + 1) * bs])
            out_ref[column, p] = value
            if p in (Q, 2 * Q + 2):
                part = pl.ds(0, Q + 1) if p == Q else pl.ds(Q + 1, Q + 2)
                send = pltpu.make_async_copy(
                    out_ref.at[column, part],
                    result_ref.at[column, part],
                    out_sem.at[column, len(sends) % 2],
                )
                send.start()
                sends.append(send)
    for send in sends:
        send.wait()


def vmem():
    return pl.BlockSpec(memory_space=pltpu.VMEM)


def smem():
    return pl.BlockSpec(memory_space=pltpu.SMEM)


def local(total, inner, hamiltonian, pattern, ortho, lists):
    local_count, _, bs = hamiltonian.shape[:3]
    slot_count = lists.shape[1]
    order = slot_count * bs
    params = pltpu.CompilerParams(vmem_limit_bytes=VMEM_LIMIT)
    band_shape = jax.ShapeDtypeStruct((2 * Q + 1, bs, bs), BF)
    orth_cols = 2 * Q + local_count
    payload = (local_count * PER, bs, bs)
    z_blocks, band0, band1, following = pl.pallas_call(
        functools.partial(main_kernel, total, inner),
        out_shape=(
            jax.ShapeDtypeStruct(((2 * REACH + 1) * local_count, 2, bs, bs), BF),
            band_shape,
            band_shape,
            band_shape,
        ),
        in_specs=[smem(), smem(), vmem(), vmem()],
        out_specs=(vmem(),) * 4,
        scratch_shapes=[
            pltpu.VMEM((2 * REACH + 1,) + payload, BF),
            pltpu.VMEM(payload, BF),
            pltpu.VMEM((orth_cols, RO + 1, bs, bs), BF),
            pltpu.VMEM((orth_cols, RO + 1, 8, bs), F32),
            pltpu.VMEM((orth_cols, bs, 2 * bs), BF),
            pltpu.VMEM((order, order), BF),
            pltpu.VMEM((order, order), BF),
            pltpu.VMEM((order, order), BF),
            pltpu.VMEM((slot_count, bs, bs), BF),
            pltpu.SemaphoreType.DMA((6, 2)),
            pltpu.SemaphoreType.DMA((2 * REACH + 1, 2)),
            pltpu.SemaphoreType.DMA((2,)),
            pltpu.SemaphoreType.DMA(((2 * REACH + 1) * local_count,)),
        ],
        compiler_params=pltpu.CompilerParams(
            collective_id=0, has_side_effects=True, vmem_limit_bytes=VMEM_LIMIT
        ),
        name="main",
    )(lists, pattern, hamiltonian, ortho)
    return pl.pallas_call(
        back_kernel,
        out_shape=jax.ShapeDtypeStruct((local_count, 2 * Q + 3, bs, bs), F32),
        in_specs=[vmem()] * 4,
        out_specs=pl.BlockSpec(memory_space=pl.ANY),
        scratch_shapes=[
            pltpu.VMEM((local_count, 2 * Q + 3, bs, bs), F32),
            pltpu.SemaphoreType.DMA((local_count, 2)),
        ],
        compiler_params=params,
        name="back",
    )(z_blocks, band0, band1, following)


def solution(mesh):
    in_specs = (
        P(AXES, None, None, None),
        P(AXES, None),
        P(AXES, None, None, None),
        P(AXES, None),
    )
    inner = mesh.shape["inner"]
    total = mesh.shape["space"] * inner
    return jax.shard_map(
        functools.partial(local, total, inner),
        mesh=mesh,
        in_specs=in_specs,
        out_specs=P(AXES, None, None, None),
        check_vma=False,
    )
```

```python
import functools
import math

import jax
import jax.numpy as jnp
from jax import lax
from jax.experimental import pallas as pl
from jax.experimental.pallas import tpu as pltpu
from jax.sharding import PartitionSpec as P

RO = 3
Q = 5
STEPS = 3
CHEM = 0.25
AXES = ("space", "inner")
MESH = pl.DeviceIdType.MESH
BF = jnp.bfloat16
F32 = jnp.float32
PER = 5
REACH = 3
HALF = 5
VMEM_LIMIT = 60 * 1024 * 1024


def exchange_parts(total, inner, g_ref, pay_ref, next_ref, band_ref, send_sem, recv_sem, band_sem):
    me = lax.axis_index("space") * inner + lax.axis_index("inner")
    core = lax.rem(me, 2)
    even = core == 0
    odd = core == 1
    chip_odd = lax.rem(me // 2, 2) == 1
    chip_even = lax.rem(me // 2, 2) == 0
    partner = me + 1 - 2 * core
    across = jnp.where(chip_odd, me - 2, me + 2)
    far = jnp.where(odd, me + 3, me - 3)
    side = jnp.where(odd, me + 1, me - 1)
    has_low = me >= 4
    has_high = me + 4 < total
    has_far = (far >= 0) & (far < total)
    has_side = (side >= 0) & (side < total)

    def place(device):
        return (device // inner, lax.rem(device, inner))

    def greet():
        barrier = pltpu.get_barrier_semaphore()

        def one(device):
            pl.semaphore_signal(barrier, inc=1, device_id=place(device), device_id_type=MESH)

        one(partner)
        one(across)
        pl.when(has_low)(lambda: one(me - 4))
        pl.when(has_high)(lambda: one(me + 4))
        pl.when(has_far)(lambda: one(far))
        pl.when(has_side)(lambda: one(side))

    def meet():
        peers = jnp.int32(2)
        for has in (has_low, has_high, has_far, has_side):
            peers = peers + has.astype(jnp.int32)
        pl.semaphore_wait(pltpu.get_barrier_semaphore(), peers)

    def clear():
        for slot in range(2 * REACH + 1):
            if slot != REACH:
                source = me + slot - REACH

                @pl.when((source < 0) | (source >= total))
                def _():
                    g_ref[slot] = jnp.zeros(g_ref.shape[1:], g_ref.dtype)

        @pl.when(me == total - 1)
        def _():
            next_ref[...] = jnp.zeros(next_ref.shape, next_ref.dtype)

    def copy(src, dst_slot, lo, hi, number, part, device):
        return pltpu.make_async_remote_copy(
            src_ref=src.at[pl.ds(lo, hi - lo)],
            dst_ref=g_ref.at[dst_slot, pl.ds(lo, hi - lo)],
            send_sem=send_sem.at[number, part],
            recv_sem=recv_sem.at[dst_slot, part],
            device_id=place(device),
            device_id_type=MESH,
        )

    whole = ((0, 0, HALF), (1, HALF, 2 * HALF))
    tail = ((0, 2, HALF), (1, HALF, 2 * HALF))
    head = ((0, 0, HALF), (1, HALF, HALF + 2))

    def copies(src, slot, number, device, pieces):
        return [copy(src, slot, lo, hi, number, part, device) for part, lo, hi in pieces]

    up = copies(pay_ref, 1, 0, across, whole)
    down = copies(pay_ref, 5, 0, across, whole)
    far_up = copies(pay_ref, 0, 1, far, tail)
    far_down = copies(pay_ref, 6, 1, far, head)
    side_up = copies(pay_ref, 2, 2, partner, whole)
    side_down = copies(pay_ref, 4, 2, partner, whole)
    relay_up = copies(g_ref.at[5], 1, 3, me + 4, whole)
    relay_down = copies(g_ref.at[1], 5, 3, me - 4, whole)
    low0 = copies(g_ref.at[1], 0, 4, partner, tail)
    low1 = copies(g_ref.at[1], 2, 4, partner, whole)
    high0 = copies(g_ref.at[5], 4, 5, partner, whole)
    high1 = copies(g_ref.at[5], 6, 5, partner, head)
    got_low = chip_odd | has_low
    got_high = chip_even | has_high

    def send():
        for part in range(2):
            pl.when(has_far & odd)(lambda: far_up[part].start())
            pl.when(has_far & even)(lambda: far_down[part].start())
            pl.when(chip_even)(lambda: up[part].start())
            pl.when(chip_odd)(lambda: down[part].start())
            pl.when(even)(lambda: side_up[part].start())
            pl.when(odd)(lambda: side_down[part].start())

    def pass_low(part):
        up[part].wait_recv()
        pl.when(chip_odd & has_low)(lambda: relay_down[part].start())
        pl.when(even)(lambda: low0[part].start())
        pl.when(odd)(lambda: low1[part].start())

    def pass_high(part):
        down[part].wait_recv()
        pl.when(chip_even & has_high)(lambda: relay_up[part].start())
        pl.when(even)(lambda: high0[part].start())
        pl.when(odd)(lambda: high1[part].start())

    def receive_low():
        for part in range(2):

            @pl.when(even)
            def _():
                pl.when(has_far)(lambda: far_up[part].wait_recv())
                pl.when(got_low)(lambda: low1[part].wait_recv())

            @pl.when(odd)
            def _():
                pl.when(got_low)(lambda: low0[part].wait_recv())
                side_up[part].wait_recv()

    def receive_high():
        for part in range(2):

            @pl.when(even)
            def _():
                side_down[part].wait_recv()
                pl.when(got_high)(lambda: high1[part].wait_recv())

            @pl.when(odd)
            def _():
                pl.when(got_high)(lambda: high0[part].wait_recv())
                pl.when(has_far)(lambda: far_down[part].wait_recv())

    def receive(orth):
        @pl.when(chip_odd)
        def _():
            for part in range(2):
                pass_low(part)
            receive_low()
            orth(range(-Q, 2), range(-Q, -1))
            for part in range(2):
                pl.when(has_high)(lambda: pass_high(part))
            receive_high()
            orth(range(2, Q + 2), range(-1, Q + 2))

        @pl.when(chip_even)
        def _():
            for part in range(2):
                pass_high(part)
            receive_high()
            orth(range(0, Q + 2), range(1, Q + 2))
            for part in range(2):
                pl.when(has_low)(lambda: pass_low(part))
            receive_low()
            orth(range(-Q, 0), range(-Q, 1))

    def drain():
        for part in range(2):

            @pl.when(even)
            def _():
                pl.when(has_far)(lambda: far_down[part].wait_send())
                side_up[part].wait_send()
                pl.when(got_low)(lambda: low0[part].wait_send())
                pl.when(got_high)(lambda: high0[part].wait_send())

            @pl.when(odd)
            def _():
                pl.when(has_far)(lambda: far_up[part].wait_send())
                side_down[part].wait_send()
                pl.when(got_low)(lambda: low1[part].wait_send())
                pl.when(got_high)(lambda: high1[part].wait_send())

            pl.when(chip_even)(lambda: up[part].wait_send())
            pl.when(chip_odd)(lambda: down[part].wait_send())
            pl.when(chip_even & has_high)(lambda: relay_up[part].wait_send())
            pl.when(chip_odd & has_low)(lambda: relay_down[part].wait_send())

    band_copy = pltpu.make_async_remote_copy(
        src_ref=band_ref,
        dst_ref=next_ref,
        send_sem=band_sem.at[0],
        recv_sem=band_sem.at[1],
        device_id=place(me - 1),
        device_id_type=MESH,
    )

    def band_send():
        pl.when(me >= 1)(lambda: band_copy.start())

    def band_wait():
        pl.when(me < total - 1)(lambda: band_copy.wait_recv())
        pl.when(me >= 1)(lambda: band_copy.wait_send())

    return me, greet, meet, clear, send, receive, drain, band_send, band_wait


def prepare(first, pattern_ref, ham_ref, ortho_ref, pay_ref, g_ref):
    bs = ham_ref.shape[-1]
    eye = jnp.where(eye_mask(bs, bs), 1.0, 0.0)
    for c in range(ham_ref.shape[0]):
        blocks = [
            jnp.where(first + c == 0, 0.0, ortho_ref[c, 0].astype(F32)),
            ortho_ref[c, 1].astype(F32) + eye,
        ]
        for r in range(3):
            keep = pattern_ref[c, r + 2].astype(F32)
            blocks.append(ham_ref[c, r + 2].astype(F32) * keep)
        for which, block in enumerate(blocks):
            block = block.astype(BF)
            pay_ref[c * PER + which] = block
            g_ref[REACH, c * PER + which] = block


def main_kernel(
    total,
    inner,
    lists_ref,
    pattern_ref,
    ham_ref,
    ortho_ref,
    z_ref,
    band0_ref,
    band1_ref,
    next_ref,
    g_ref,
    pay_ref,
    h_ref,
    sq_ref,
    zt_ref,
    x_ref,
    m_ref,
    y_ref,
    pc_ref,
    send_sem,
    recv_sem,
    band_sem,
    z_sem,
):
    me, greet, meet, clear, send, receive, drain, band_send, band_wait = exchange_parts(
        total, inner, g_ref, pay_ref, next_ref, band0_ref, send_sem, recv_sem, band_sem
    )
    first = me * lists_ref.shape[0]
    greet()
    prepare(first, pattern_ref, ham_ref, ortho_ref, pay_ref, g_ref)
    clear()
    meet()
    send()
    receive(functools.partial(orth_stage, g_ref, h_ref, sq_ref, zt_ref))
    z_copies = []
    for column in range(1, z_ref.shape[0]):
        block = g_ref.at[column // 2, pl.ds((column % 2) * PER, 2)]
        z_copies.append(pltpu.make_async_copy(block, z_ref.at[column], z_sem.at[column]))
        z_copies[-1].start()
    work = (x_ref, m_ref, y_ref, pc_ref)
    assemble(0, lists_ref, first, h_ref, sq_ref, x_ref)
    iterate(0, lists_ref, first, band0_ref, *work)
    band_send()
    assemble(1, lists_ref, first, h_ref, sq_ref, x_ref)
    iterate(1, lists_ref, first, band1_ref, *work)
    drain()
    for z_copy in z_copies:
        z_copy.wait()
    band_wait()


def block_of(g_ref, column, which):
    index = column + 2 * REACH
    return g_ref[index // 2, (index % 2) * PER + which]


def dot(left, right):
    return jnp.dot(left, right, preferred_element_type=F32)


def eye_mask(rows, columns, shift=0):
    row = lax.broadcasted_iota(jnp.int32, (rows, columns), 0) + shift
    return row == lax.broadcasted_iota(jnp.int32, (rows, columns), 1)


def fold(square):
    n = square.shape[0]
    return jnp.sum(square.reshape(n // 8, 8, square.shape[1]), axis=0)


def orth_stage(g_ref, h_ref, sq_ref, zt_ref, rows_here, columns_here):
    bs = g_ref.shape[-1]
    last = Q + 1
    quarter = jnp.where(eye_mask(bs, bs), CHEM, 0.0)
    for a in rows_here:
        zt_ref[a + Q] = jnp.concatenate(
            [block_of(g_ref, a, 0).T, block_of(g_ref, a, 1).T], axis=1
        )
    for b in columns_here:
        count = min(RO + 1, last - b + 1)
        z_col = jnp.concatenate([block_of(g_ref, b, 0), block_of(g_ref, b, 1)], axis=0)
        below = block_of(g_ref, b - 1, 3)
        rows = [jnp.concatenate([block_of(g_ref, b - 1, 2), below.T], axis=1)]
        rows.append(jnp.concatenate([below, block_of(g_ref, b, 2)], axis=1))
        if count >= 2:
            rows.append(jnp.concatenate([block_of(g_ref, b - 1, 4), block_of(g_ref, b, 3)], axis=1))
        product = dot(jnp.concatenate(rows, axis=0), z_col).astype(BF)
        if count >= 3:
            tail = dot(block_of(g_ref, b, 4), z_col[bs:]).astype(BF)
            product = jnp.concatenate([product, tail], axis=0)
        for off in range(count):
            transposed = zt_ref[b + off + Q]
            if off < RO:
                value = dot(transposed, product[off * bs : (off + 2) * bs])
            else:
                value = dot(transposed[:, :bs], product[off * bs : (off + 1) * bs])
            value = value.astype(BF)
            h_ref[b + Q, off] = value
            wide = value.astype(F32)
            if off == 0:
                wide = quarter - wide
            sq_ref[b + Q, off] = fold(wide * wide)


def assemble(which, lists_ref, first, h_ref, sq_ref, x_ref):
    bs = h_ref.shape[-1]
    slot_count = lists_ref.shape[1]
    slots = [lists_ref[which, s] for s in range(slot_count)]
    live = [slot >= 0 for slot in slots]
    place = [jnp.clip(slot - first + Q, 0, 2 * Q + 1) for slot in slots]
    total = jnp.zeros((8, bs), F32)
    live_count = jnp.int32(0)
    pick = {}
    for s in range(slot_count):
        live_count = live_count + live[s].astype(jnp.int32)
        for t in range(s + 1):
            low = jnp.minimum(place[s], place[t])
            off = jnp.maximum(place[s], place[t]) - low
            valid = live[s] & live[t] & (off <= RO)
            off = jnp.minimum(off, RO)
            pick[s, t] = (low, off, valid)
            part = jnp.where(valid, sq_ref[low, off], 0.0)
            total = total + (part if s == t else 2.0 * part)
    total = jnp.sum(jnp.sum(total, axis=1, keepdims=True), axis=0, keepdims=True)
    rows = jnp.full((1, 1), live_count * bs, jnp.int32).astype(F32)
    scale = 2.0 * jnp.sqrt(total / rows + 1e-06)
    inverse = 1.0 / scale
    eye = eye_mask(bs, bs)
    for s in range(slot_count):
        for t in range(s + 1):
            low, off, valid = pick[s, t]
            value = h_ref[low, off].astype(F32)
            if s == t:
                value = jnp.where(eye, CHEM, 0.0) - value
            else:
                value = -value
            value = jnp.where(valid, value * inverse, 0.0)
            here, there = pl.ds(s * bs, bs), pl.ds(t * bs, bs)
            if s == t:
                x_ref[here, here] = value.astype(BF)
            else:
                flipped = value.T
                straight = place[s] >= place[t]
                x_ref[here, there] = jnp.where(straight, value, flipped).astype(BF)
                x_ref[there, here] = jnp.where(straight, flipped, value).astype(BF)


def iterate(which, lists_ref, first, band_ref, x_ref, m_ref, y_ref, pc_ref):
    bs = pc_ref.shape[-1]
    slot_count = lists_ref.shape[1]
    order = slot_count * bs
    chunk = math.gcd(order, 256)
    source, target = x_ref, y_ref

    def mirrored(out_ref, at, value):
        width = value.shape[1]
        out_ref[pl.ds(at, chunk), :width] = value.astype(BF)
        for left in range(0, at, chunk):
            flipped = value[:, left : left + chunk].T
            out_ref[pl.ds(left, chunk), pl.ds(at, chunk)] = flipped.astype(BF)

    for step in range(STEPS - 1):
        for at in range(0, order, chunk):
            width = at + chunk
            square = dot(source[pl.ds(at, chunk), :], source[:, :width])
            unit = jnp.where(eye_mask(chunk, width, at), 1.5, 0.0)
            mirrored(m_ref, at, unit - 0.5 * square)
        for at in range(0, order, chunk):
            mirrored(target, at, dot(source[pl.ds(at, chunk), :], m_ref[:, : at + chunk]))
        source, target = target, source
    columns = source[:, :bs]
    for at in range(0, order, chunk):
        square = dot(source[pl.ds(at, chunk), :], columns)
        unit = jnp.where(eye_mask(chunk, bs, at), 1.5, 0.0)
        m_ref[pl.ds(at, chunk), :bs] = (unit - 0.5 * square).astype(BF)
    factor = m_ref[:, :bs]
    for s in range(slot_count):
        result = dot(source[pl.ds(s * bs, bs), :], factor)
        if s == 0:
            result = result + jnp.where(eye_mask(bs, bs), 1.0, 0.0)
        pc_ref[s] = (0.5 * result).astype(BF)
    for r in range(2 * Q + 1):
        at = jnp.int32(0)
        found = jnp.bool_(False)
        for s in range(slot_count):
            slot = lists_ref[which, s]
            hit = (slot >= 0) & (slot == first + which + r - Q)
            at = jnp.where(hit, s, at)
            found = found | hit
        band_ref[r] = jnp.where(found, pc_ref[at], jnp.zeros((bs, bs), BF))


def back_kernel(z_ref, band0_ref, band1_ref, next_ref, result_ref, out_ref, out_sem):
    bs = z_ref.shape[-1]
    zero = jnp.zeros((bs, bs), BF)

    def z_of(column, which):
        return z_ref[column + 2 * REACH, which]

    sends = []
    for column in range(2):
        mine = (band0_ref, band1_ref)[column]
        after = (band1_ref, next_ref)[column]
        right = jnp.concatenate(
            [z_of(column, 1).T, z_of(column + 1, 0).T], axis=0
        )
        rows = []
        for i in range(2 * Q + 2):
            here = mine[i] if i <= 2 * Q else zero
            there = after[i - 1] if i >= 1 else zero
            rows.append(jnp.concatenate([here, there], axis=1))
        y = dot(jnp.concatenate(rows, axis=0), right).astype(BF)
        for p in range(2 * Q + 3):
            a = column + p - Q - 1
            if p == 0:
                value = dot(z_of(a + 1, 0), y[:bs])
            elif p == 2 * Q + 2:
                value = dot(z_of(a, 1), y[(p - 1) * bs : p * bs])
            else:
                left = jnp.concatenate(
                    [z_of(a, 1), z_of(a + 1, 0)], axis=1
                )
                value = dot(left, y[(p - 1) * bs : (p + 1) * bs])
            out_ref[column, p] = value
            if p in (Q, 2 * Q + 2):
                part = pl.ds(0, Q + 1) if p == Q else pl.ds(Q + 1, Q + 2)
                send = pltpu.make_async_copy(
                    out_ref.at[column, part],
                    result_ref.at[column, part],
                    out_sem.at[column, len(sends) % 2],
                )
                send.start()
                sends.append(send)
    for send in sends:
        send.wait()


def vmem():
    return pl.BlockSpec(memory_space=pltpu.VMEM)


def smem():
    return pl.BlockSpec(memory_space=pltpu.SMEM)


def local(total, inner, hamiltonian, pattern, ortho, lists):
    local_count, _, bs = hamiltonian.shape[:3]
    slot_count = lists.shape[1]
    order = slot_count * bs
    params = pltpu.CompilerParams(vmem_limit_bytes=VMEM_LIMIT)
    band_shape = jax.ShapeDtypeStruct((2 * Q + 1, bs, bs), BF)
    orth_cols = 2 * Q + local_count
    payload = (local_count * PER, bs, bs)
    z_blocks, band0, band1, following = pl.pallas_call(
        functools.partial(main_kernel, total, inner),
        out_shape=(
            jax.ShapeDtypeStruct(((2 * REACH + 1) * local_count, 2, bs, bs), BF),
            band_shape,
            band_shape,
            band_shape,
        ),
        in_specs=[smem(), smem(), vmem(), vmem()],
        out_specs=(vmem(),) * 4,
        scratch_shapes=[
            pltpu.VMEM((2 * REACH + 1,) + payload, BF),
            pltpu.VMEM(payload, BF),
            pltpu.VMEM((orth_cols, RO + 1, bs, bs), BF),
            pltpu.VMEM((orth_cols, RO + 1, 8, bs), F32),
            pltpu.VMEM((orth_cols, bs, 2 * bs), BF),
            pltpu.VMEM((order, order), BF),
            pltpu.VMEM((order, order), BF),
            pltpu.VMEM((order, order), BF),
            pltpu.VMEM((slot_count, bs, bs), BF),
            pltpu.SemaphoreType.DMA((6, 2)),
            pltpu.SemaphoreType.DMA((2 * REACH + 1, 2)),
            pltpu.SemaphoreType.DMA((2,)),
            pltpu.SemaphoreType.DMA(((2 * REACH + 1) * local_count,)),
        ],
        compiler_params=pltpu.CompilerParams(
            collective_id=0, has_side_effects=True, vmem_limit_bytes=VMEM_LIMIT
        ),
        name="main",
    )(lists, pattern, hamiltonian, ortho)
    return pl.pallas_call(
        back_kernel,
        out_shape=jax.ShapeDtypeStruct((local_count, 2 * Q + 3, bs, bs), F32),
        in_specs=[vmem()] * 4,
        out_specs=pl.BlockSpec(memory_space=pl.ANY),
        scratch_shapes=[
            pltpu.VMEM((local_count, 2 * Q + 3, bs, bs), F32),
            pltpu.SemaphoreType.DMA((local_count, 2)),
        ],
        compiler_params=params,
        name="back",
    )(z_blocks, band0, band1, following)


def solution(mesh):
    in_specs = (
        P(AXES, None, None, None),
        P(AXES, None),
        P(AXES, None, None, None),
        P(AXES, None),
    )
    inner = mesh.shape["inner"]
    total = mesh.shape["space"] * inner
    return jax.shard_map(
        functools.partial(local, total, inner),
        mesh=mesh,
        in_specs=in_specs,
        out_specs=P(AXES, None, None, None),
        check_vma=False,
    )
```
